32 devices in a mesh: rows: 4 (over y, x), cols: 8 (over z, core).
Axes of the slice: x: 2, y: 2, z: 4, core: 2. Of those that a mesh axis runs over, the one named last changes fastest.
Arguments:
- heat_excess: float32 [8, 1024, 4096], P(None, ('rows', 'cols')), may hold values from -6 to 6
- square_region_label: int32 [1024, 4096], P(('rows', 'cols')), may hold values from 0 to 63
- region_heating_flux: float32 [64], replicated, may hold values from 0.05 to 0.5
- layer_substance_label: int32 [8], replicated, may hold values from 0 to 3, as said below
- sideways_coupling_factor: float32 [4], replicated, may hold values from 0.08 to 0.2
- upward_coupling_factor: float32 [4], replicated, may hold values from 0.02 to 0.08
- layer_heating_fraction: float32 [4], replicated, may hold values from 0.1 to 0.6
Outputs:
- ending_heat_excess: float32 [8, 1024, 4096], P(None, 'rows', 'cols')
The draws below stay inside these ranges and needn't reach their ends.
Inputs may be any that keep to these rules, and one draw needn't show every extreme that they name: `layer_substance_label`: each material is named by exactly 2 tiers.
All inputs are finite; a program needn't handle non-finite values.
Results may differ from the reference program's by a relative error of at most 0.00002.
Values sent between devices are 32-bit elements; how exact they have to be, the bound alone decides.
A program may use at most 192 MiB of HBM per device.

```python
import math
import jax
import jax.numpy as jnp
from jax import lax

LAYER_COUNT = 8
NMAT = 4
NBLOCKS = 64
EPOCH_TOTAL = 8
MESH_HEIGHTWISE = 1024
MESH_WIDTHWISE = 4096


def draw_layer_substance_label(key, part):
    pieces = [jax.random.permutation(jax.random.fold_in(key, 7 + index), NMAT) for index in range(LAYER_COUNT // NMAT)]
    return jnp.concatenate(pieces).astype(jnp.int32)


def set_ends(entries, stream_key, least, top_value):
    index_at = [jax.random.randint(jax.random.fold_in(stream_key, axis), (), 0, length) for axis, length in enumerate(entries.shape)]
    longest = entries.shape.index(max(entries.shape))
    beside = index_at[:longest] + [(index_at[longest] + 1) % entries.shape[longest]] + index_at[longest + 1:]
    return entries.at[tuple(index_at)].set(least).at[tuple(beside)].set(top_value)


def levels(key, shape, shards, least, high):
    loudness, own = 1.0, jax.random.fold_in(key, 6)
    for dim, shards_of in shards:
        steps = jnp.exp(jax.random.uniform(jax.random.fold_in(own, dim), (shards_of,), jnp.float32, least / len(shards), high / len(shards)))
        loudness = loudness * jnp.repeat(steps, shape[dim] // shards_of).reshape([-1 if axis == dim else 1 for axis in range(len(shape))])
    return loudness


def centred(stream_key, dims, scale, most, cuts=(), dtype=jnp.bfloat16):
    drawn = jax.random.normal(stream_key, dims, jnp.float32) * scale
    if len(cuts) > 0:
        drawn = levels(stream_key, dims, cuts, -0.22, 0.18) * drawn
    return jnp.clip(drawn, min=-most, max=most).astype(dtype)


def setup_inputs(seed: int = 0) -> dict:
    key_of = jax.random.split(jax.random.key(seed), 8)
    heat_excess = centred(key_of[0], (LAYER_COUNT, MESH_HEIGHTWISE, MESH_WIDTHWISE), 1.0, 6.0, ((1, 32),), jnp.float32)
    square_region_label = set_ends(jax.random.randint(key_of[1], (MESH_HEIGHTWISE, MESH_WIDTHWISE), 0, NBLOCKS), jax.random.fold_in(key_of[1], 1), 0, NBLOCKS - 1).astype(jnp.int32)
    region_heating_flux = jnp.clip(jnp.exp(jax.random.uniform(key_of[2], (NBLOCKS,), jnp.float32, math.log(0.05), math.log(0.5))), 0.05, 0.5)
    layer_substance_label = draw_layer_substance_label(jax.random.fold_in(key_of[7], 71), 0)
    sideways_coupling_factor = jnp.clip(jax.random.uniform(key_of[4], (NMAT,), jnp.float32, 0.08, 0.2), 0.08, 0.2)
    upward_coupling_factor = jnp.clip(jax.random.uniform(key_of[5], (NMAT,), jnp.float32, 0.02, 0.08), 0.02, 0.08)
    layer_heating_fraction = jnp.clip(jax.random.uniform(key_of[6], (NMAT,), jnp.float32, 0.1, 0.6), 0.1, 0.6)
    return {"heat_excess": heat_excess, "square_region_label": square_region_label, "region_heating_flux": region_heating_flux, "layer_substance_label": layer_substance_label, "sideways_coupling_factor": sideways_coupling_factor, "upward_coupling_factor": upward_coupling_factor, "layer_heating_fraction": layer_heating_fraction}


def reference(heat_excess, square_region_label, region_heating_flux, layer_substance_label, sideways_coupling_factor, upward_coupling_factor, layer_heating_fraction):
    density = jnp.take(region_heating_flux, square_region_label, axis=0)
    lateral = jnp.take(sideways_coupling_factor, layer_substance_label, axis=0)[:, None, None]
    vertical = jnp.take(upward_coupling_factor, layer_substance_label, axis=0)[:, None, None]
    share = jnp.take(layer_heating_fraction, layer_substance_label, axis=0)[:, None, None]
    source = share * density[None]

    def advance_integrator(field, discarded_output):
        padded = jnp.pad(field, ((0, 0), (1, 1), (1, 1)))
        beside = padded[:, 2:, 1:-1] + padded[:, :-2, 1:-1]
        beside = beside + padded[:, 1:-1, 2:] + padded[:, 1:-1, :-2]
        above = jnp.concatenate([field[1:], jnp.zeros_like(field[:1])], axis=0)
        flux = vertical * (above - field)
        below = jnp.concatenate([jnp.zeros_like(flux[:1]), flux[:-1]], axis=0)
        fresh = field + lateral * (beside - 4.0 * field) + flux - below + source
        return fresh, None

    ending_heat_excess, discarded_output = lax.scan(advance_integrator, heat_excess, None, length=EPOCH_TOTAL)
    return ending_heat_excess
```

```python
import jax
import jax.numpy as jnp
from jax import lax
from jax.experimental import pallas as pl
from jax.experimental.pallas import tpu as pltpu
from jax.sharding import PartitionSpec as P

EPOCH_TOTAL = 8
HALO = 8
LANES = 128


def kernel(
    rows,
    cols,
    heat,
    label,
    flux_tab,
    tier_lab,
    lat_tab,
    vert_tab,
    share_tab,
    out,
    ext,
    lab_ext,
    dens,
    buf,
    mask,
    res,
    in_sem,
    halo_send,
    halo_recv,
    send_sem,
    recv_sem,
    own_sem,
):
    tiers, height, breadth = heat.shape
    tall = height + 2 * HALO
    width = breadth // cols
    wide = width + 2 * LANES
    r = lax.axis_index("rows")
    c = lax.axis_index("cols")
    me = r * cols + c
    total = rows * cols
    has_prev = me > 0
    has_next = me < total - 1
    prev = lax.rem(me + total - 1, total)
    nxt = lax.rem(me + 1, total)
    prev_id = (prev // cols, lax.rem(prev, cols))
    next_id = (nxt // cols, lax.rem(nxt, cols))
    MESH = pl.DeviceIdType.MESH

    own_heat = pltpu.make_async_copy(
        heat, ext.at[:, pl.ds(HALO, height), pl.ds(LANES, breadth)], in_sem.at[0]
    )
    own_heat.start()
    own_lab = pltpu.make_async_copy(
        label, lab_ext.at[pl.ds(HALO, height), pl.ds(LANES, breadth)], in_sem.at[1]
    )
    own_lab.start()

    barrier = pltpu.get_barrier_semaphore()
    for j in range(1, cols):
        pl.semaphore_signal(
            barrier, inc=1, device_id=(r, lax.rem(c + j, cols)), device_id_type=MESH
        )
    far_prev = has_prev & (c == 0)
    far_next = has_next & (c == cols - 1)

    @pl.when(far_prev)
    def _():
        pl.semaphore_signal(barrier, inc=1, device_id=prev_id, device_id_type=MESH)

    @pl.when(far_next)
    def _():
        pl.semaphore_signal(barrier, inc=1, device_id=next_id, device_id_type=MESH)

    pl.semaphore_wait(
        barrier, cols - 1 + far_prev.astype(jnp.int32) + far_next.astype(jnp.int32)
    )

    inner = pl.ds(LANES, breadth)
    top, bottom = pl.ds(0, HALO), pl.ds(HALO + height, HALO)

    def halo(src_rows, dst_rows, where, slot):
        return (
            pltpu.make_async_remote_copy(
                src_ref=heat.at[:, src_rows, :],
                dst_ref=ext.at[:, dst_rows, inner],
                send_sem=halo_send.at[2 * slot],
                recv_sem=halo_recv.at[2 * slot],
                device_id=where,
                device_id_type=MESH,
            ),
            pltpu.make_async_remote_copy(
                src_ref=label.at[src_rows, :],
                dst_ref=lab_ext.at[dst_rows, inner],
                send_sem=halo_send.at[2 * slot + 1],
                recv_sem=halo_recv.at[2 * slot + 1],
                device_id=where,
                device_id_type=MESH,
            ),
        )

    down = halo(pl.ds(height - HALO, HALO), top, next_id, 0)
    up = halo(pl.ds(0, HALO), bottom, prev_id, 1)

    @pl.when(has_next)
    def _():
        for copy in down:
            copy.start()

    @pl.when(has_prev)
    def _():
        for copy in up:
            copy.start()

    @pl.when(jnp.logical_not(has_prev))
    def _():
        ext[:, 0:HALO, :] = jnp.zeros((tiers, HALO, breadth + 2 * LANES), jnp.float32)
        lab_ext[0:HALO, :] = jnp.zeros((HALO, breadth + 2 * LANES), jnp.int32)

    @pl.when(jnp.logical_not(has_next))
    def _():
        ext[:, HALO + height :, :] = jnp.zeros(
            (tiers, HALO, breadth + 2 * LANES), jnp.float32
        )
        lab_ext[HALO + height :, :] = jnp.zeros(
            (HALO, breadth + 2 * LANES), jnp.int32
        )

    for at in (0, LANES + breadth):
        ext[:, HALO : HALO + height, at : at + LANES] = jnp.zeros(
            (tiers, height, LANES), jnp.float32
        )
        dens[:, at : at + LANES] = jnp.zeros((tall, LANES), jnp.float32)

    @pl.when(has_prev)
    def _():
        for at in (0, LANES + breadth):
            ext[:, 0:HALO, at : at + LANES] = jnp.zeros(
                (tiers, HALO, LANES), jnp.float32
            )

    @pl.when(has_next)
    def _():
        for at in (0, LANES + breadth):
            ext[:, HALO + height :, at : at + LANES] = jnp.zeros(
                (tiers, HALO, LANES), jnp.float32
            )

    blocks = flux_tab.shape[0]
    piece = 4 * LANES

    def look_up(first, count):
        def one(i, carry):
            at = pl.ds(pl.multiple_of(LANES + i * piece, LANES), piece)
            ids = lab_ext[first : first + count, at]
            found = jnp.zeros((count, piece), jnp.float32)
            for b in range(blocks):
                found = jnp.where(ids == b, flux_tab[b], found)
            dens[first : first + count, at] = found
            return carry

        lax.fori_loop(0, breadth // piece, one, 0)

    own_lab.wait()
    for first in range(HALO, HALO + height, HALO):
        look_up(first, HALO)

    @pl.when(has_prev)
    def _():
        for copy in down:
            copy.wait_recv()

    @pl.when(has_next)
    def _():
        for copy in up:
            copy.wait_recv()

    look_up(0, HALO)
    look_up(HALO + height, HALO)
    own_heat.wait()

    lat = [lat_tab[tier_lab[k]] for k in range(tiers)]
    vert = [vert_tab[tier_lab[k]] for k in range(tiers)]
    share = [share_tab[tier_lab[k]] for k in range(tiers)]

    def send(dest):
        return pltpu.make_async_remote_copy(
            src_ref=res.at[dest],
            dst_ref=out.at[:, pl.ds(pl.multiple_of(c * height, HALO), height), :],
            send_sem=send_sem.at[dest],
            recv_sem=recv_sem.at[c],
            device_id=(r, dest),
            device_id_type=MESH,
        )

    def compute(dest):
        base = pl.multiple_of(dest * width, LANES)
        window = pl.ds(base, wide)
        row_pos = me * height - HALO + lax.broadcasted_iota(jnp.int32, (tall, wide), 0)
        col_pos = base - LANES + lax.broadcasted_iota(jnp.int32, (tall, wide), 1)
        ok = (row_pos >= 0) & (row_pos < total * height)
        ok = ok & (col_pos >= 0) & (col_pos < breadth)
        mask[...] = jnp.where(ok, 1.0, 0.0)

        def step(read, store):
            for g in range(tall // HALO):
                lo = g * HALO
                here = slice(lo, lo + HALO)
                before = slice(max(lo - HALO, 0), max(lo - HALO, 0) + HALO)
                last = min(lo + HALO, tall - HALO)
                after = slice(last, last + HALO)
                power = dens[here, window]
                inside = mask[here, :]
                edge = lax.broadcasted_iota(jnp.int32, (HALO, wide), 0)
                centre = read(0, here)
                flux_below = None
                for k in range(tiers):
                    above = read(k + 1, here) if k + 1 < tiers else None
                    north = jnp.where(
                        edge == 0,
                        pltpu.roll(read(k, before), 1, 0),
                        pltpu.roll(centre, 1, 0),
                    )
                    south = jnp.where(
                        edge == HALO - 1,
                        pltpu.roll(read(k, after), HALO - 1, 0),
                        pltpu.roll(centre, HALO - 1, 0),
                    )
                    beside = north + south
                    beside = beside + pltpu.roll(centre, 1, 1)
                    beside = beside + pltpu.roll(centre, wide - 1, 1)
                    rise = -centre if above is None else above - centre
                    flux = vert[k] * rise
                    fresh = centre * (1.0 - 4.0 * lat[k]) + lat[k] * beside
                    fresh = fresh + flux
                    if flux_below is not None:
                        fresh = fresh - flux_below
                    fresh = fresh + share[k] * power
                    store(k, here, fresh * inside)
                    flux_below = flux
                    centre = above

        def from_buf(which):
            return lambda k, at: buf[which, k, at, :]

        def to_buf(which):
            def put(k, at, value):
                buf[which, k, at, :] = value

            return put

        def load(k, carry):
            buf[0, k] = ext[k, :, window]
            return carry

        lax.fori_loop(0, tiers, load, 0)

        def pair(i, carry):
            step(from_buf(0), to_buf(1))
            step(from_buf(1), to_buf(0))
            return carry

        lax.fori_loop(0, EPOCH_TOTAL // 2, pair, 0)

        def keep(k, carry):
            res[dest, k] = buf[0, k, HALO : HALO + height, LANES : LANES + width]
            return carry

        lax.fori_loop(0, tiers, keep, 0)

    half = max(cols // 2, 1)
    side = c // half

    def dest_of(i):
        far = lax.rem(side + 1, 2) * half + lax.rem(c + i, half)
        j = i - half
        quarter = half // 2
        late = jnp.where(j < half - 1, j - (half - quarter) + 1, 0)
        off = jnp.where(j < half - quarter, j + quarter, late)
        near = side * half + lax.rem(c + off, half)
        return jnp.where(i < half, far, near)

    def one_chunk(i, carry):
        dest = dest_of(i)
        compute(dest)
        send(dest).start()
        return carry

    lax.fori_loop(0, cols - 1, one_chunk, 0)
    compute(c)
    own = pltpu.make_async_copy(
        res.at[c],
        out.at[:, pl.ds(pl.multiple_of(c * height, HALO), height), :],
        own_sem.at[0],
    )
    own.start()

    @pl.when(has_next)
    def _():
        for copy in down:
            copy.wait_send()

    @pl.when(has_prev)
    def _():
        for copy in up:
            copy.wait_send()

    def finish(j, carry):
        other = lax.rem(c + j, cols)
        pltpu.make_async_remote_copy(
            src_ref=res.at[other],
            dst_ref=out.at[:, pl.ds(pl.multiple_of(other * height, HALO), height), :],
            send_sem=send_sem.at[other],
            recv_sem=recv_sem.at[other],
            device_id=(r, other),
            device_id_type=MESH,
        ).wait()
        return carry

    lax.fori_loop(1, cols, finish, 0)
    own.wait()


def solution(mesh):
    rows, cols = mesh.shape["rows"], mesh.shape["cols"]

    def body(heat, label, flux_tab, tier_lab, lat_tab, vert_tab, share_tab):
        tiers, height, breadth = heat.shape
        tall = height + 2 * HALO
        width = breadth // cols
        wide = width + 2 * LANES
        smem = pl.BlockSpec(memory_space=pltpu.SMEM)
        hbm = pl.BlockSpec(memory_space=pl.ANY)
        dma = pltpu.SemaphoreType.DMA

        def run(*refs):
            kernel(rows, cols, *refs)

        return pl.pallas_call(
            run,
            out_shape=jax.ShapeDtypeStruct((tiers, height * cols, width), jnp.float32),
            in_specs=[hbm, hbm, smem, smem, smem, smem, smem],
            out_specs=hbm,
            scratch_shapes=[
                pltpu.VMEM((tiers, tall, breadth + 2 * LANES), jnp.float32),
                pltpu.VMEM((tall, breadth + 2 * LANES), jnp.int32),
                pltpu.VMEM((tall, breadth + 2 * LANES), jnp.float32),
                pltpu.VMEM((2, tiers, tall, wide), jnp.float32),
                pltpu.VMEM((tall, wide), jnp.float32),
                pltpu.VMEM((cols, tiers, height, width), jnp.float32),
                dma((2,)),
                dma((4,)),
                dma((4,)),
                dma((cols,)),
                dma((cols,)),
                dma((1,)),
            ],
            compiler_params=pltpu.CompilerParams(
                collective_id=0, has_side_effects=True, vmem_limit_bytes=48 * 2**20
            ),
        )(heat, label, flux_tab, tier_lab, lat_tab, vert_tab, share_tab)

    return jax.shard_map(
        body,
        mesh=mesh,
        in_specs=(
            P(None, ("rows", "cols"), None),
            P(("rows", "cols"), None),
            P(),
            P(),
            P(),
            P(),
            P(),
        ),
        out_specs=P(None, "rows", "cols"),
        check_vma=False,
    )
```

```python
import jax
import jax.numpy as jnp
from jax import lax
from jax.experimental import pallas as pl
from jax.experimental.pallas import tpu as pltpu
from jax.sharding import PartitionSpec as P

EPOCH_TOTAL = 8
HALO = 8
LANES = 128


def kernel(
    rows,
    cols,
    heat,
    label,
    flux_tab,
    tier_lab,
    lat_tab,
    vert_tab,
    share_tab,
    out,
    ext,
    lab_ext,
    dens,
    buf,
    mask,
    res,
    in_sem,
    halo_send,
    halo_recv,
    send_sem,
    recv_sem,
    own_sem,
):
    tiers, height, breadth = heat.shape
    tall = height + 2 * HALO
    width = breadth // cols
    wide = width + 2 * LANES
    r = lax.axis_index("rows")
    c = lax.axis_index("cols")
    me = r * cols + c
    total = rows * cols
    has_prev = me > 0
    has_next = me < total - 1
    prev = lax.rem(me + total - 1, total)
    nxt = lax.rem(me + 1, total)
    prev_id = (prev // cols, lax.rem(prev, cols))
    next_id = (nxt // cols, lax.rem(nxt, cols))
    MESH = pl.DeviceIdType.MESH

    own_heat = pltpu.make_async_copy(
        heat, ext.at[:, pl.ds(HALO, height), pl.ds(LANES, breadth)], in_sem.at[0]
    )
    own_heat.start()
    own_lab = pltpu.make_async_copy(
        label, lab_ext.at[pl.ds(HALO, height), pl.ds(LANES, breadth)], in_sem.at[1]
    )
    own_lab.start()

    barrier = pltpu.get_barrier_semaphore()
    for j in range(1, cols):
        pl.semaphore_signal(
            barrier, inc=1, device_id=(r, lax.rem(c + j, cols)), device_id_type=MESH
        )
    far_prev = has_prev & (c == 0)
    far_next = has_next & (c == cols - 1)

    @pl.when(far_prev)
    def _():
        pl.semaphore_signal(barrier, inc=1, device_id=prev_id, device_id_type=MESH)

    @pl.when(far_next)
    def _():
        pl.semaphore_signal(barrier, inc=1, device_id=next_id, device_id_type=MESH)

    pl.semaphore_wait(
        barrier, cols - 1 + far_prev.astype(jnp.int32) + far_next.astype(jnp.int32)
    )

    top, bottom = (0, HALO), (HALO + height, HALO)
    half = max(cols // 2, 1)
    middle = half * width
    side = c // half

    def spans(device):
        low_first = device // half
        first = (1 - low_first) * (middle - LANES)
        rest = low_first * (middle + LANES)
        return (first, middle + LANES), (rest, breadth - middle - LANES)

    def halo(src_row, dst_rows, where, slot, span):
        start, size = span
        start = pl.multiple_of(start, LANES)
        src = (pl.ds(src_row, HALO), pl.ds(start, size))
        dst = (
            pl.ds(dst_rows[0], dst_rows[1]),
            pl.ds(pl.multiple_of(start + LANES, LANES), size),
        )
        return (
            pltpu.make_async_remote_copy(
                src_ref=heat.at[:, src[0], src[1]],
                dst_ref=ext.at[:, dst[0], dst[1]],
                send_sem=halo_send.at[2 * slot],
                recv_sem=halo_recv.at[2 * slot],
                device_id=where,
                device_id_type=MESH,
            ),
            pltpu.make_async_remote_copy(
                src_ref=label.at[src[0], src[1]],
                dst_ref=lab_ext.at[dst[0], dst[1]],
                send_sem=halo_send.at[2 * slot + 1],
                recv_sem=halo_recv.at[2 * slot + 1],
                device_id=where,
                device_id_type=MESH,
            ),
        )

    def down(i, device):
        return halo(height - HALO, top, next_id, i, spans(device)[i])

    def up(i, device):
        return halo(0, bottom, prev_id, 2 + i, spans(device)[i])

    for i in range(2):

        @pl.when(has_next)
        def _():
            for copy in reversed(down(i, next_id[1])):
                copy.start()

        @pl.when(has_prev)
        def _():
            for copy in reversed(up(i, prev_id[1])):
                copy.start()

    @pl.when(jnp.logical_not(has_prev))
    def _():
        ext[:, 0:HALO, :] = jnp.zeros((tiers, HALO, breadth + 2 * LANES), jnp.float32)
        lab_ext[0:HALO, :] = jnp.zeros((HALO, breadth + 2 * LANES), jnp.int32)

    @pl.when(jnp.logical_not(has_next))
    def _():
        ext[:, HALO + height :, :] = jnp.zeros(
            (tiers, HALO, breadth + 2 * LANES), jnp.float32
        )
        lab_ext[HALO + height :, :] = jnp.zeros(
            (HALO, breadth + 2 * LANES), jnp.int32
        )

    for at in (0, LANES + breadth):
        ext[:, HALO : HALO + height, at : at + LANES] = jnp.zeros(
            (tiers, height, LANES), jnp.float32
        )
        dens[:, at : at + LANES] = jnp.zeros((tall, LANES), jnp.float32)

    @pl.when(has_prev)
    def _():
        for at in (0, LANES + breadth):
            ext[:, 0:HALO, at : at + LANES] = jnp.zeros(
                (tiers, HALO, LANES), jnp.float32
            )

    @pl.when(has_next)
    def _():
        for at in (0, LANES + breadth):
            ext[:, HALO + height :, at : at + LANES] = jnp.zeros(
                (tiers, HALO, LANES), jnp.float32
            )

    blocks = flux_tab.shape[0]
    piece = 4 * LANES

    def look_up(at, first, count):
        ids = lab_ext[first : first + count, at]
        found = jnp.zeros(ids.shape, jnp.float32)
        for b in range(blocks):
            found = jnp.where(ids == b, flux_tab[b], found)
        dens[first : first + count, at] = found

    def own_density(i, carry):
        at = pl.ds(pl.multiple_of(LANES + i * piece, LANES), piece)
        for first in range(HALO, HALO + height, HALO):
            look_up(at, first, HALO)
        return carry

    own_lab.wait()
    lax.fori_loop(0, breadth // piece, own_density, 0)
    own_heat.wait()

    def take_halo(i):
        @pl.when(has_prev)
        def _():
            for copy in down(i, c):
                copy.wait_recv()

        @pl.when(has_next)
        def _():
            for copy in up(i, c):
                copy.wait_recv()

        start, size = spans(c)[i]

        def one(j, carry):
            at = pl.ds(pl.multiple_of(LANES + start + j * LANES, LANES), LANES)
            look_up(at, 0, HALO)
            look_up(at, HALO + height, HALO)
            return carry

        lax.fori_loop(0, size // LANES, one, 0)

    lat = [lat_tab[tier_lab[k]] for k in range(tiers)]
    vert = [vert_tab[tier_lab[k]] for k in range(tiers)]
    share = [share_tab[tier_lab[k]] for k in range(tiers)]

    def send(dest):
        return pltpu.make_async_remote_copy(
            src_ref=res.at[dest],
            dst_ref=out.at[:, pl.ds(pl.multiple_of(c * height, HALO), height), :],
            send_sem=send_sem.at[dest],
            recv_sem=recv_sem.at[c],
            device_id=(r, dest),
            device_id_type=MESH,
        )

    def compute(dest):
        base = pl.multiple_of(dest * width, LANES)
        window = pl.ds(base, wide)
        row_pos = me * height - HALO + lax.broadcasted_iota(jnp.int32, (tall, wide), 0)
        col_pos = base - LANES + lax.broadcasted_iota(jnp.int32, (tall, wide), 1)
        ok = (row_pos >= 0) & (row_pos < total * height)
        ok = ok & (col_pos >= 0) & (col_pos < breadth)
        mask[...] = jnp.where(ok, 1.0, 0.0)

        def step(read, store):
            for g in range(tall // HALO):
                lo = g * HALO
                here = slice(lo, lo + HALO)
                before = slice(max(lo - HALO, 0), max(lo - HALO, 0) + HALO)
                last = min(lo + HALO, tall - HALO)
                after = slice(last, last + HALO)
                power = dens[here, window]
                inside = mask[here, :]
                edge = lax.broadcasted_iota(jnp.int32, (HALO, wide), 0)
                centre = read(0, here)
                flux_below = None
                for k in range(tiers):
                    above = read(k + 1, here) if k + 1 < tiers else None
                    north = jnp.where(
                        edge == 0,
                        pltpu.roll(read(k, before), 1, 0),
                        pltpu.roll(centre, 1, 0),
                    )
                    south = jnp.where(
                        edge == HALO - 1,
                        pltpu.roll(read(k, after), HALO - 1, 0),
                        pltpu.roll(centre, HALO - 1, 0),
                    )
                    beside = north + south
                    beside = beside + pltpu.roll(centre, 1, 1)
                    beside = beside + pltpu.roll(centre, wide - 1, 1)
                    rise = -centre if above is None else above - centre
                    flux = vert[k] * rise
                    fresh = centre * (1.0 - 4.0 * lat[k]) + lat[k] * beside
                    fresh = fresh + flux
                    if flux_below is not None:
                        fresh = fresh - flux_below
                    fresh = fresh + share[k] * power
                    store(k, here, fresh * inside)
                    flux_below = flux
                    centre = above

        def from_buf(which):
            return lambda k, at: buf[which, k, at, :]

        def to_buf(which):
            def put(k, at, value):
                buf[which, k, at, :] = value

            return put

        def load(k, carry):
            buf[0, k] = ext[k, :, window]
            return carry

        lax.fori_loop(0, tiers, load, 0)

        def pair(i, carry):
            step(from_buf(0), to_buf(1))
            step(from_buf(1), to_buf(0))
            return carry

        lax.fori_loop(0, EPOCH_TOTAL // 2, pair, 0)

        def keep(k, carry):
            res[dest, k] = buf[0, k, HALO : HALO + height, LANES : LANES + width]
            return carry

        lax.fori_loop(0, tiers, keep, 0)

    def dest_of(i):
        far = lax.rem(side + 1, 2) * half + lax.rem(c + i, half)
        j = i - half
        quarter = half // 2
        late = jnp.where(j < half - 1, j - (half - quarter) + 1, 0)
        off = jnp.where(j < half - quarter, j + quarter, late)
        near = side * half + lax.rem(c + off, half)
        return jnp.where(i < half, far, near)

    def one_chunk(i, carry):
        dest = dest_of(i)
        compute(dest)
        send(dest).start()
        return carry

    take_halo(0)
    lax.fori_loop(0, half, one_chunk, 0)
    take_halo(1)
    lax.fori_loop(half, cols - 1, one_chunk, 0)
    compute(c)
    own = pltpu.make_async_copy(
        res.at[c],
        out.at[:, pl.ds(pl.multiple_of(c * height, HALO), height), :],
        own_sem.at[0],
    )
    own.start()

    for i in range(2):

        @pl.when(has_next)
        def _():
            for copy in down(i, next_id[1]):
                copy.wait_send()

        @pl.when(has_prev)
        def _():
            for copy in up(i, prev_id[1]):
                copy.wait_send()

    def finish(j, carry):
        other = lax.rem(c + j, cols)
        pltpu.make_async_remote_copy(
            src_ref=res.at[other],
            dst_ref=out.at[:, pl.ds(pl.multiple_of(other * height, HALO), height), :],
            send_sem=send_sem.at[other],
            recv_sem=recv_sem.at[other],
            device_id=(r, other),
            device_id_type=MESH,
        ).wait()
        return carry

    lax.fori_loop(1, cols, finish, 0)
    own.wait()


def solution(mesh):
    rows, cols = mesh.shape["rows"], mesh.shape["cols"]

    def body(heat, label, flux_tab, tier_lab, lat_tab, vert_tab, share_tab):
        tiers, height, breadth = heat.shape
        tall = height + 2 * HALO
        width = breadth // cols
        wide = width + 2 * LANES
        smem = pl.BlockSpec(memory_space=pltpu.SMEM)
        hbm = pl.BlockSpec(memory_space=pl.ANY)
        dma = pltpu.SemaphoreType.DMA

        def run(*refs):
            kernel(rows, cols, *refs)

        return pl.pallas_call(
            run,
            out_shape=jax.ShapeDtypeStruct((tiers, height * cols, width), jnp.float32),
            in_specs=[hbm, hbm, smem, smem, smem, smem, smem],
            out_specs=hbm,
            scratch_shapes=[
                pltpu.VMEM((tiers, tall, breadth + 2 * LANES), jnp.float32),
                pltpu.VMEM((tall, breadth + 2 * LANES), jnp.int32),
                pltpu.VMEM((tall, breadth + 2 * LANES), jnp.float32),
                pltpu.VMEM((2, tiers, tall, wide), jnp.float32),
                pltpu.VMEM((tall, wide), jnp.float32),
                pltpu.VMEM((cols, tiers, height, width), jnp.float32),
                dma((2,)),
                dma((8,)),
                dma((8,)),
                dma((cols,)),
                dma((cols,)),
                dma((1,)),
            ],
            compiler_params=pltpu.CompilerParams(
                collective_id=0, has_side_effects=True, vmem_limit_bytes=48 * 2**20
            ),
        )(heat, label, flux_tab, tier_lab, lat_tab, vert_tab, share_tab)

    return jax.shard_map(
        body,
        mesh=mesh,
        in_specs=(
            P(None, ("rows", "cols"), None),
            P(("rows", "cols"), None),
            P(),
            P(),
            P(),
            P(),
            P(),
        ),
        out_specs=P(None, "rows", "cols"),
        check_vma=False,
    )
```

```python
import jax
import jax.numpy as jnp
from jax import lax
from jax.experimental import pallas as pl
from jax.experimental.pallas import tpu as pltpu
from jax.sharding import PartitionSpec as P

EPOCH_TOTAL = 8
HALO = 8
LANES = 128


def kernel(
    rows,
    cols,
    heat,
    label,
    flux_src,
    tier_src,
    lat_src,
    vert_src,
    share_src,
    out,
    ext,
    lab_ext,
    dens,
    buf,
    mask,
    res,
    in_sem,
    halo_send,
    halo_recv,
    send_sem,
    recv_sem,
    own_sem,
    flux_tab,
    tier_lab,
    lat_tab,
    vert_tab,
    share_tab,
    small_sem,
):
    tiers, height, breadth = heat.shape
    tall = height + 2 * HALO
    width = breadth // cols
    wide = width + 2 * LANES
    r = lax.axis_index("rows")
    c = lax.axis_index("cols")
    me = r * cols + c
    total = rows * cols
    has_prev = me > 0
    has_next = me < total - 1
    prev = lax.rem(me + total - 1, total)
    nxt = lax.rem(me + 1, total)
    prev_id = (prev // cols, lax.rem(prev, cols))
    next_id = (nxt // cols, lax.rem(nxt, cols))
    MESH = pl.DeviceIdType.MESH

    own_heat = pltpu.make_async_copy(
        heat, ext.at[:, pl.ds(HALO, height), pl.ds(LANES, breadth)], in_sem.at[0]
    )
    own_heat.start()
    own_lab = pltpu.make_async_copy(
        label, lab_ext.at[pl.ds(HALO, height), pl.ds(LANES, breadth)], in_sem.at[1]
    )
    own_lab.start()

    small = [
        pltpu.make_async_copy(src, dst, small_sem.at[i])
        for i, (src, dst) in enumerate(
            (
                (flux_src, flux_tab),
                (tier_src, tier_lab),
                (lat_src, lat_tab),
                (vert_src, vert_tab),
                (share_src, share_tab),
            )
        )
    ]
    for copy in small:
        copy.start()

    barrier = pltpu.get_barrier_semaphore()
    for j in range(1, cols):
        pl.semaphore_signal(
            barrier, inc=1, device_id=(r, lax.rem(c + j, cols)), device_id_type=MESH
        )
    far_prev = has_prev & (c == 0)
    far_next = has_next & (c == cols - 1)

    @pl.when(far_prev)
    def _():
        pl.semaphore_signal(barrier, inc=1, device_id=prev_id, device_id_type=MESH)

    @pl.when(far_next)
    def _():
        pl.semaphore_signal(barrier, inc=1, device_id=next_id, device_id_type=MESH)

    pl.semaphore_wait(
        barrier, cols - 1 + far_prev.astype(jnp.int32) + far_next.astype(jnp.int32)
    )

    top, bottom = (0, HALO), (HALO + height, HALO)
    half = max(cols // 2, 1)
    middle = half * width
    side = c // half

    def spans(device):
        low_first = device // half
        first = (1 - low_first) * (middle - LANES)
        rest = low_first * (middle + LANES)
        return (first, middle + LANES), (rest, breadth - middle - LANES)

    def halo(src_row, dst_rows, where, slot, span):
        start, size = span
        start = pl.multiple_of(start, LANES)
        src = (pl.ds(src_row, HALO), pl.ds(start, size))
        dst = (
            pl.ds(dst_rows[0], dst_rows[1]),
            pl.ds(pl.multiple_of(start + LANES, LANES), size),
        )
        return (
            pltpu.make_async_remote_copy(
                src_ref=heat.at[:, src[0], src[1]],
                dst_ref=ext.at[:, dst[0], dst[1]],
                send_sem=halo_send.at[2 * slot],
                recv_sem=halo_recv.at[2 * slot],
                device_id=where,
                device_id_type=MESH,
            ),
            pltpu.make_async_remote_copy(
                src_ref=label.at[src[0], src[1]],
                dst_ref=lab_ext.at[dst[0], dst[1]],
                send_sem=halo_send.at[2 * slot + 1],
                recv_sem=halo_recv.at[2 * slot + 1],
                device_id=where,
                device_id_type=MESH,
            ),
        )

    def down(i, device):
        return halo(height - HALO, top, next_id, i, spans(device)[i])

    def up(i, device):
        return halo(0, bottom, prev_id, 2 + i, spans(device)[i])

    for i in range(2):

        @pl.when(has_next)
        def _():
            for copy in reversed(down(i, next_id[1])):
                copy.start()

        @pl.when(has_prev)
        def _():
            for copy in reversed(up(i, prev_id[1])):
                copy.start()

    @pl.when(jnp.logical_not(has_prev))
    def _():
        ext[:, 0:HALO, :] = jnp.zeros((tiers, HALO, breadth + 2 * LANES), jnp.float32)
        lab_ext[0:HALO, :] = jnp.zeros((HALO, breadth + 2 * LANES), jnp.int32)

    @pl.when(jnp.logical_not(has_next))
    def _():
        ext[:, HALO + height :, :] = jnp.zeros(
            (tiers, HALO, breadth + 2 * LANES), jnp.float32
        )
        lab_ext[HALO + height :, :] = jnp.zeros(
            (HALO, breadth + 2 * LANES), jnp.int32
        )

    for at in (0, LANES + breadth):
        ext[:, HALO : HALO + height, at : at + LANES] = jnp.zeros(
            (tiers, height, LANES), jnp.float32
        )
        dens[:, at : at + LANES] = jnp.zeros((tall, LANES), jnp.float32)

    @pl.when(has_prev)
    def _():
        for at in (0, LANES + breadth):
            ext[:, 0:HALO, at : at + LANES] = jnp.zeros(
                (tiers, HALO, LANES), jnp.float32
            )

    @pl.when(has_next)
    def _():
        for at in (0, LANES + breadth):
            ext[:, HALO + height :, at : at + LANES] = jnp.zeros(
                (tiers, HALO, LANES), jnp.float32
            )

    blocks = flux_tab.shape[0]
    piece = 4 * LANES

    def look_up(at, first, count):
        ids = lab_ext[first : first + count, at]
        found = jnp.zeros(ids.shape, jnp.float32)
        for b in range(blocks):
            found = jnp.where(ids == b, flux_tab[b], found)
        dens[first : first + count, at] = found

    def own_density(i, carry):
        at = pl.ds(pl.multiple_of(LANES + i * piece, LANES), piece)
        for first in range(HALO, HALO + height, HALO):
            look_up(at, first, HALO)
        return carry

    for copy in small:
        copy.wait()
    own_lab.wait()
    lax.fori_loop(0, breadth // piece, own_density, 0)
    own_heat.wait()

    def take_halo(i):
        @pl.when(has_prev)
        def _():
            for copy in down(i, c):
                copy.wait_recv()

        @pl.when(has_next)
        def _():
            for copy in up(i, c):
                copy.wait_recv()

        start, size = spans(c)[i]

        def one(j, carry):
            at = pl.ds(pl.multiple_of(LANES + start + j * LANES, LANES), LANES)
            look_up(at, 0, HALO)
            look_up(at, HALO + height, HALO)
            return carry

        lax.fori_loop(0, size // LANES, one, 0)

    lat = [lat_tab[tier_lab[k]] for k in range(tiers)]
    vert = [vert_tab[tier_lab[k]] for k in range(tiers)]
    share = [share_tab[tier_lab[k]] for k in range(tiers)]

    def send(dest):
        return pltpu.make_async_remote_copy(
            src_ref=res.at[dest],
            dst_ref=out.at[:, pl.ds(pl.multiple_of(c * height, HALO), height), :],
            send_sem=send_sem.at[dest],
            recv_sem=recv_sem.at[c],
            device_id=(r, dest),
            device_id_type=MESH,
        )

    def compute(dest):
        base = pl.multiple_of(dest * width, LANES)
        window = pl.ds(base, wide)
        row_pos = me * height - HALO + lax.broadcasted_iota(jnp.int32, (tall, wide), 0)
        col_pos = base - LANES + lax.broadcasted_iota(jnp.int32, (tall, wide), 1)
        ok = (row_pos >= 0) & (row_pos < total * height)
        ok = ok & (col_pos >= 0) & (col_pos < breadth)
        mask[...] = jnp.where(ok, 1.0, 0.0)

        def step(read, store):
            for g in range(tall // HALO):
                lo = g * HALO
                here = slice(lo, lo + HALO)
                before = slice(max(lo - HALO, 0), max(lo - HALO, 0) + HALO)
                last = min(lo + HALO, tall - HALO)
                after = slice(last, last + HALO)
                power = dens[here, window]
                inside = mask[here, :]
                edge = lax.broadcasted_iota(jnp.int32, (HALO, wide), 0)
                centre = read(0, here)
                flux_below = None
                for k in range(tiers):
                    above = read(k + 1, here) if k + 1 < tiers else None
                    north = jnp.where(
                        edge == 0,
                        pltpu.roll(read(k, before), 1, 0),
                        pltpu.roll(centre, 1, 0),
                    )
                    south = jnp.where(
                        edge == HALO - 1,
                        pltpu.roll(read(k, after), HALO - 1, 0),
                        pltpu.roll(centre, HALO - 1, 0),
                    )
                    beside = north + south
                    beside = beside + pltpu.roll(centre, 1, 1)
                    beside = beside + pltpu.roll(centre, wide - 1, 1)
                    rise = -centre if above is None else above - centre
                    flux = vert[k] * rise
                    fresh = centre * (1.0 - 4.0 * lat[k]) + lat[k] * beside
                    fresh = fresh + flux
                    if flux_below is not None:
                        fresh = fresh - flux_below
                    fresh = fresh + share[k] * power
                    store(k, here, fresh * inside)
                    flux_below = flux
                    centre = above

        def from_buf(which):
            return lambda k, at: buf[which, k, at, :]

        def to_buf(which):
            def put(k, at, value):
                buf[which, k, at, :] = value

            return put

        def load(k, carry):
            buf[0, k] = ext[k, :, window]
            return carry

        lax.fori_loop(0, tiers, load, 0)

        def pair(i, carry):
            step(from_buf(0), to_buf(1))
            step(from_buf(1), to_buf(0))
            return carry

        lax.fori_loop(0, EPOCH_TOTAL // 2, pair, 0)

        def keep(k, carry):
            res[dest, k] = buf[0, k, HALO : HALO + height, LANES : LANES + width]
            return carry

        lax.fori_loop(0, tiers, keep, 0)

    def dest_of(i):
        far = lax.rem(side + 1, 2) * half + lax.rem(c + i, half)
        j = i - half
        quarter = half // 2
        late = jnp.where(j < half - 1, j - (half - quarter) + 1, 0)
        off = jnp.where(j < half - quarter, j + quarter, late)
        near = side * half + lax.rem(c + off, half)
        return jnp.where(i < half, far, near)

    def one_chunk(i, carry):
        dest = dest_of(i)
        compute(dest)
        send(dest).start()
        return carry

    take_halo(0)
    lax.fori_loop(0, half, one_chunk, 0)
    take_halo(1)
    lax.fori_loop(half, cols - 1, one_chunk, 0)
    compute(c)
    own = pltpu.make_async_copy(
        res.at[c],
        out.at[:, pl.ds(pl.multiple_of(c * height, HALO), height), :],
        own_sem.at[0],
    )
    own.start()

    for i in range(2):

        @pl.when(has_next)
        def _():
            for copy in down(i, next_id[1]):
                copy.wait_send()

        @pl.when(has_prev)
        def _():
            for copy in up(i, prev_id[1]):
                copy.wait_send()

    def finish(j, carry):
        other = lax.rem(c + j, cols)
        pltpu.make_async_remote_copy(
            src_ref=res.at[other],
            dst_ref=out.at[:, pl.ds(pl.multiple_of(other * height, HALO), height), :],
            send_sem=send_sem.at[other],
            recv_sem=recv_sem.at[other],
            device_id=(r, other),
            device_id_type=MESH,
        ).wait()
        return carry

    lax.fori_loop(1, cols, finish, 0)
    own.wait()


def solution(mesh):
    rows, cols = mesh.shape["rows"], mesh.shape["cols"]

    def body(heat, label, flux_tab, tier_lab, lat_tab, vert_tab, share_tab):
        tiers, height, breadth = heat.shape
        tall = height + 2 * HALO
        width = breadth // cols
        wide = width + 2 * LANES
        hbm = pl.BlockSpec(memory_space=pl.ANY)
        dma = pltpu.SemaphoreType.DMA

        def run(*refs):
            kernel(rows, cols, *refs)

        return pl.pallas_call(
            run,
            out_shape=jax.ShapeDtypeStruct((tiers, height * cols, width), jnp.float32),
            in_specs=[hbm] * 7,
            out_specs=hbm,
            scratch_shapes=[
                pltpu.VMEM((tiers, tall, breadth + 2 * LANES), jnp.float32),
                pltpu.VMEM((tall, breadth + 2 * LANES), jnp.int32),
                pltpu.VMEM((tall, breadth + 2 * LANES), jnp.float32),
                pltpu.VMEM((2, tiers, tall, wide), jnp.float32),
                pltpu.VMEM((tall, wide), jnp.float32),
                pltpu.VMEM((cols, tiers, height, width), jnp.float32),
                dma((2,)),
                dma((8,)),
                dma((8,)),
                dma((cols,)),
                dma((cols,)),
                dma((1,)),
                *[
                    pltpu.SMEM(x.shape, x.dtype)
                    for x in (flux_tab, tier_lab, lat_tab, vert_tab, share_tab)
                ],
                dma((5,)),
            ],
            compiler_params=pltpu.CompilerParams(
                collective_id=0, has_side_effects=True, vmem_limit_bytes=48 * 2**20
            ),
        )(heat, label, flux_tab, tier_lab, lat_tab, vert_tab, share_tab)

    return jax.shard_map(
        body,
        mesh=mesh,
        in_specs=(
            P(None, ("rows", "cols"), None),
            P(("rows", "cols"), None),
            P(),
            P(),
            P(),
            P(),
            P(),
        ),
        out_specs=P(None, "rows", "cols"),
        check_vma=False,
    )
```
